512 devices in a mesh: layer: 128 (over z, x, core), tile: 4 (over y).
Axes of the slice: x: 4, y: 4, z: 16, core: 2. Of those that a mesh axis runs over, the one named last changes fastest.
Arguments:
- sources: float32 [128, 2, 2, 32, 8192], P('layer', None, None, None, 'tile'), may hold values from -6 to 6
- green: float32 [128, 80, 2, 128, 128], P('layer', 'tile'), may hold values from -0.25 to 0.25
- rowcol: int32 [128, 80, 2], P('layer', 'tile'), may hold values from 0 to 63, as said below
- counts: int32 [128, 16], P('layer', 'tile'), may hold values from 1 to 5, as said below
Outputs:
- traces: float32 [128, 2, 2, 32, 8192], P('layer', None, None, None, 'tile')
The draws below stay inside these ranges and needn't reach their ends.
Inputs may be any that keep to these rules, and one draw needn't show every extreme that they name: `rowcol`: the row tile of a slot of tile device t lies in t * 16 to (t + 1) * 16 - 1; its column tile differs from its row tile by at most 4. Kind 0 has 2 or more live slots; the four counts of one tile device sum to at most 10; in every layer some tile device has 5 live slots of kind 0 and 10 live slots in all.
All inputs are finite; a program needn't handle non-finite values.
Results may differ from the reference program's by a relative error of at most 0.0003.
Values sent between devices are 32-bit elements; how exact they have to be, the bound alone decides.
A program may use at most 64 MiB of HBM per device.

```python
import jax
import jax.numpy as jnp
from jax import lax

IFACE = 8192
TILE = 128
SHOTS = 32
CAP = 5
BAND = 4
TICKS = 6
LAYERS = 128
TILES = 64
TILES_DEV = 16
SLOTS = 80


def draw_rowcol(key, part):
    first_key, second_key = jax.random.split(jax.random.fold_in(key, 11))
    slot = jnp.arange(SLOTS, dtype=jnp.int32)
    owner = slot // (4 * CAP)
    first = owner * TILES_DEV
    quarter = slot % (4 * CAP)
    row = first[None, :] + jax.random.randint(first_key, (LAYERS, SLOTS), 0, TILES_DEV, dtype=jnp.int32)
    offset = jax.random.randint(second_key, (LAYERS, SLOTS), -BAND, BAND + 1, dtype=jnp.int32)
    row = jnp.where(quarter[None, :] == 0, first[None, :], row)
    row = jnp.where(quarter[None, :] == 1, first[None, :] + TILES_DEV - 1, row)
    offset = jnp.where(quarter[None, :] == 0, -BAND, offset)
    offset = jnp.where(quarter[None, :] == 1, BAND, offset)
    column = jnp.clip(row + offset, 0, TILES - 1)
    return jnp.stack([row, column], axis=-1).astype(jnp.int32)


def draw_counts(key, part):
    keys = jax.random.split(jax.random.fold_in(key, 23), 4)
    devices = SLOTS // CAP // 4
    kind_zero = jax.random.randint(keys[0], (LAYERS, devices, 1), 2, CAP + 1, dtype=jnp.int32)
    room = (2 * CAP - kind_zero) // 3
    spread = jax.random.randint(keys[1], (LAYERS, devices, 3), 0, CAP, dtype=jnp.int32)
    others = 1 + spread % room
    normal_rows = jnp.concatenate([kind_zero, others], axis=-1)
    chosen = jax.random.randint(keys[2], (LAYERS, 1, 1), 0, 3, dtype=jnp.int32)
    lanes = jnp.arange(3, dtype=jnp.int32)[None, None, :]
    busy_others = 1 + jnp.where(lanes == chosen, CAP - 3, 0)
    busy_row = jnp.concatenate([jnp.full((LAYERS, 1, 1), CAP, jnp.int32), busy_others], axis=-1)
    busiest = jax.random.randint(keys[3], (LAYERS, 1, 1), 0, devices, dtype=jnp.int32)
    device_index = jnp.arange(devices, dtype=jnp.int32)[None, :, None]
    result = jnp.where(device_index == busiest, busy_row, normal_rows)
    return result.reshape(LAYERS, 4 * devices).astype(jnp.int32)


def levels(rng, dims, shards, smallest, largest):
    def one(position, parts):
        steps = jax.random.uniform(jax.random.fold_in(jax.random.fold_in(rng, 6), position), (parts,), jnp.float32, smallest / len(shards), largest / len(shards))
        return jnp.repeat(jnp.exp(steps), dims[position] // parts).reshape((-1,) + (1,) * (len(dims) - position - 1))

    loudness = one(*shards[0])
    for cut in shards[1:]:
        loudness = loudness * one(*cut)
    return loudness


def normal_values(stream_key, shape, width, bound, cuts=(), held_as=jnp.bfloat16):
    loudness = levels(stream_key, shape, cuts, -0.22, 0.18) if cuts else 1.0
    array = jax.random.normal(stream_key, shape, jnp.float32) * width * loudness
    return jnp.minimum(jnp.maximum(array, -bound), bound).astype(held_as)


def setup_inputs(seed: int = 0) -> dict:
    arg_keys = jax.random.split(jax.random.key(seed), 5)
    sources = normal_values(arg_keys[0], (LAYERS, 2, 2, SHOTS, IFACE), 1.0, 6.0, ((0, 128), (4, 4)), jnp.float32)
    green = normal_values(arg_keys[1], (LAYERS, SLOTS, 2, TILE, TILE), (4 * TILE) ** -0.5, 0.25, ((0, 128), (1, 4)), jnp.float32)
    rowcol = draw_rowcol(jax.random.fold_in(arg_keys[4], 71), 0)
    counts = draw_counts(jax.random.fold_in(arg_keys[4], 71), 0)
    return dict(sources=sources, green=green, rowcol=rowcol, counts=counts)


def apply_layer(prev_down, next_up, blocks, pairs, live_counts):
    slot = jnp.arange(SLOTS, dtype=jnp.int32)
    group = slot // CAP
    kind = group % 4
    live = ((slot % CAP) < live_counts[group]).astype(jnp.float32)
    anchor = jnp.where((kind == 1) | (kind == 2), 1, 0).astype(jnp.int32)
    source = jnp.stack([prev_down, next_up]).reshape(2, 2, SHOTS, TILES, TILE)
    picked = source[anchor, :, :, pairs[:, 1]]
    prod = jnp.einsum('ncsj,ndij->ncdsi', picked, blocks, precision=lax.Precision.HIGHEST)
    real = prod[:, 0, 0] - prod[:, 1, 1]
    imag = prod[:, 0, 1] + prod[:, 1, 0]
    terms = jnp.stack([real, imag], axis=1) * live[:, None, None, None]
    target = (jnp.where(kind < 2, 0, 1) * TILES + pairs[:, 0]).astype(jnp.int32)
    summed = jax.ops.segment_sum(terms, target, num_segments=2 * TILES)
    summed = summed.reshape(2, TILES, 2, SHOTS, TILE).transpose(0, 2, 3, 1, 4)
    return summed.reshape(2, 2, SHOTS, IFACE)


def reference(sources, green, rowcol, counts):
    traces = jnp.zeros_like(sources)
    for sweep in range(TICKS):
        down = traces[:, 0]
        upward = traces[:, 1]
        prev_down = jnp.concatenate([jnp.zeros_like(down[:1]), down[:-1]], axis=0)
        next_up = jnp.concatenate([upward[1:], jnp.zeros_like(upward[:1])], axis=0)
        update = lax.map(lambda items: apply_layer(*items), (prev_down, next_up, green, rowcol, counts))
        traces = sources + update
    return traces
```

```python
import functools

import jax
import jax.numpy as jnp
from jax import lax
from jax.experimental import pallas as pl
from jax.experimental.pallas import tpu as pltpu
from jax.sharding import PartitionSpec as P

TILE = 128
CAP = 5
BAND = 4
SWEEPS = 5
TILES_DEV = 16
LIVE = 10
OWN = (8, 7)
GROUP = 8
SRC = LIVE
MESH = pl.DeviceIdType.MESH
F32 = jnp.float32
BF16 = jnp.bfloat16


def reader_columns(meta, first_kind, second_kind, count):
    starts = [meta[2 * LIVE * 2 + k] for k in (first_kind, second_kind)]
    columns = []
    for e in range(count):
        in_first = e < starts[0]
        slot_first = first_kind * CAP + min(e, CAP - 1)
        slot_second = second_kind * CAP + jnp.clip(e - starts[0], 0, CAP - 1)
        slot = jnp.where(in_first, slot_first, slot_second)
        columns.append(meta[2 * slot + 1])
    return columns


def kernel(
    layers,
    tile_devs,
    groups,
    meta,
    src_hbm,
    green_hbm,
    out_hbm,
    state,
    recv,
    send,
    stage,
    weights,
    green,
    final,
    meta_next,
    meta_prev,
    slot_of,
    entry_of,
    source_of,
    same,
    where_is,
    pack_of,
    local_sem,
    out_sem,
    meta_send_sem,
    meta_recv_sem,
    send_sem,
    recv_sem,
):
    layer = lax.axis_index("layer")
    place = lax.axis_index("tile")
    up_ok, down_ok = layer > 0, layer < layers - 1
    low_ok, high_ok = place > 0, place < tile_devs - 1

    src_copies = []
    for direction in range(2):
        for tile in range(TILES_DEV):
            copy = pltpu.make_async_copy(
                src_hbm.at[direction, :, :, pl.ds(tile * TILE, TILE)],
                state.at[SRC + direction * TILES_DEV + tile],
                local_sem.at[direction * TILES_DEV + tile],
            )
            copy.start()
            src_copies.append(copy)
    green_copy = pltpu.make_async_copy(green_hbm, green, local_sem.at[2 * TILES_DEV])
    green_copy.start()

    @pl.when(layer == 0)
    def _():
        @pl.loop(0, SWEEPS * groups)
        def _(i):
            recv[i // groups, i % groups, pl.ds(0, 16)] = jnp.zeros((16, 2, GROUP, TILE), F32)

    @pl.when(layer == layers - 1)
    def _():
        @pl.loop(0, SWEEPS * groups)
        def _(i):
            recv[i // groups, i % groups, pl.ds(16, 16)] = jnp.zeros((16, 2, GROUP, TILE), F32)

    lower, upper = layer + 1, layer - 1
    links = [
        (down_ok, (lower, place), up_ok),
        (down_ok & low_ok, (lower, place - 1), up_ok & high_ok),
        (down_ok & high_ok, (lower, place + 1), up_ok & low_ok),
        (up_ok, (upper, place), down_ok),
        (up_ok & low_ok, (upper, place - 1), down_ok & high_ok),
        (up_ok & high_ok, (upper, place + 1), down_ok & low_ok),
    ]

    barrier = pltpu.get_barrier_semaphore()
    for ok, device, _ in links:

        @pl.when(ok)
        def _(device=device):
            pl.semaphore_signal(barrier, inc=1, device_id=device, device_id_type=MESH)

    sides = 1 + low_ok.astype(jnp.int32) + high_ok.astype(jnp.int32)
    ends = up_ok.astype(jnp.int32) + down_ok.astype(jnp.int32)
    pl.semaphore_wait(barrier, sides * ends)

    to_prev = pltpu.make_async_remote_copy(
        meta, meta_next, meta_send_sem.at[0], meta_recv_sem.at[0], device_id=(upper, place), device_id_type=MESH
    )
    to_next = pltpu.make_async_remote_copy(
        meta, meta_prev, meta_send_sem.at[1], meta_recv_sem.at[1], device_id=(lower, place), device_id_type=MESH
    )

    @pl.when(up_ok)
    def _():
        to_prev.start()

    @pl.when(down_ok)
    def _():
        to_next.start()

    def message(k, g, q):
        direction, kind = q // 3, q % 3
        base = direction * 16
        count = OWN[direction] if kind == 0 else BAND
        if kind == 0:
            source = send.at[k, g, pl.ds(base, count)]
            target = base
        elif kind == 1:
            source = send.at[k, g, pl.ds(base + 8, count)]
            target = base + 12
        else:
            source = send.at[k, g, pl.ds(base + 12, count)]
            target = base + 8
        return pltpu.make_async_remote_copy(
            source,
            recv.at[k, g, pl.ds(target, count)],
            send_sem.at[k, g, q],
            recv_sem.at[k, g, q],
            device_id=links[q][1],
            device_id_type=MESH,
        )

    def first_halo(g, q):
        direction, kind = q // 3, q % 3
        base = direction * 16
        tile = SRC + base + (0 if kind == 1 else TILES_DEV - BAND)
        target = base + (12 if kind == 1 else 8)
        return pltpu.make_async_remote_copy(
            state.at[pl.ds(tile, BAND), :, pl.ds(pl.multiple_of(g * GROUP, GROUP), GROUP), :],
            recv.at[0, g, pl.ds(target, BAND)],
            send_sem.at[0, g, q],
            recv_sem.at[0, g, q],
            device_id=links[q][1],
            device_id_type=MESH,
        )

    for copy in src_copies:
        copy.wait()
    for g in range(groups):
        for q in (1, 2, 4, 5):

            @pl.when(links[q][0])
            def _(g=g, q=q):
                first_halo(g, q).start()

    c0, c1, c2, c3 = [meta[2 * LIVE * 2 + k] for k in range(4)]
    p1, p2, p3 = c0, c0 + c1, c0 + c1 + c2
    total = p3 + c3
    targets, lives = [], []
    for j in range(LIVE):
        in1, in2, in3 = j >= p1, j >= p2, j >= p3
        kind = in1.astype(jnp.int32) + in2.astype(jnp.int32) + in3.astype(jnp.int32)
        base = jnp.where(in3, p3, jnp.where(in2, p2, jnp.where(in1, p1, 0)))
        live = j < total
        slot = jnp.where(live, kind * CAP + j - base, 0)
        row = meta[2 * slot] - place * TILES_DEV
        col = meta[2 * slot + 1] - place * TILES_DEV
        reads_up = in1 & jnp.logical_not(in3)
        own = j - base + jnp.where(in3, c0, jnp.where(in2, c1, 0))
        entry = jnp.where(col < 0, 8 + BAND + col, jnp.where(col >= TILES_DEV, 12 + col - TILES_DEV, own))
        entry = entry + jnp.where(reads_up, 16, 0)
        target = row + jnp.where(in2, TILES_DEV, 0)
        slot_of[j] = slot
        entry_of[j] = jnp.where(live, entry, 0)
        source_of[j] = SRC + jnp.where(live, target, 0)
        targets.append(jnp.where(live, target, 64 + j))
        lives.append(live)
    for j in range(LIVE):
        same[j, j] = jnp.where(lives[j], 1.0, 0.0)
        for i in range(j):
            same[j, i] = jnp.where(targets[j] == targets[i], 1.0, 0.0)
    for r in range(2 * TILES_DEV):
        found = SRC + r
        for j in range(LIVE):
            found = jnp.where(targets[j] == r, j, found)
        where_is[r] = found

    @pl.when(up_ok)
    def _():
        to_prev.wait_send()
        to_next_recv = pltpu.make_async_remote_copy(
            meta, meta_prev, meta_send_sem.at[1], meta_recv_sem.at[1], device_id=(upper, place), device_id_type=MESH
        )
        to_next_recv.wait_recv()
        for e, column in enumerate(reader_columns(meta_prev, 1, 2, OWN[1])):
            pack_of[16 + e] = TILES_DEV + jnp.clip(column - place * TILES_DEV, 0, TILES_DEV - 1)

    @pl.when(down_ok)
    def _():
        to_next.wait_send()
        to_prev_recv = pltpu.make_async_remote_copy(
            meta, meta_next, meta_send_sem.at[0], meta_recv_sem.at[0], device_id=(lower, place), device_id_type=MESH
        )
        to_prev_recv.wait_recv()
        for e, column in enumerate(reader_columns(meta_next, 0, 3, OWN[0])):
            pack_of[e] = jnp.clip(column - place * TILES_DEV, 0, TILES_DEV - 1)

    def shots_of(g):
        return pl.ds(pl.multiple_of(g * GROUP, GROUP), GROUP)

    def pack_own(k, g, index_of):
        for direction, ok in ((0, down_ok), (1, up_ok)):

            @pl.when(ok)
            def _(direction=direction):
                for e in range(OWN[direction]):
                    i = direction * 16 + e
                    send[k, g, i] = state[index_of(pack_of[i]), :, shots_of(g), :]
                message(k, g, direction * 3).start()

    @pl.loop(0, groups)
    def _(g):
        pack_own(0, g, lambda tile: SRC + tile)

    green_copy.wait()

    @pl.loop(0, LIVE)
    def _(j):
        blocks = green[slot_of[j]] * jnp.where(j < total, 1.0, 0.0)
        re, im = blocks[0], blocks[1]
        for part, (row, col) in ((re, (0, 0)), (-im, (0, 1)), (im, (1, 0)), (re, (1, 1))):
            high = part.astype(BF16)
            low = (part - high.astype(F32)).astype(BF16)
            weights[j, pl.ds(row * TILE, TILE), pl.ds(col * TILE, TILE)] = high
            weights[j, pl.ds((2 + row) * TILE, TILE), pl.ds(col * TILE, TILE)] = low

    def step(k, g):
        for q in range(6):

            @pl.when(links[q][2])
            def _(q=q):
                message(k, g, q).wait_recv()

        stage[...] = recv[k, g]
        terms = []
        for j in range(LIVE):
            x = stage[entry_of[j]]
            x = jnp.concatenate([x[0], x[1]], axis=1)
            high = x.astype(BF16).astype(F32)
            both = jnp.concatenate([high, x - high], axis=0).astype(BF16)
            p = lax.dot_general(both, weights[j], (((1,), (1,)), ((), ())), preferred_element_type=F32)
            p = p[:, : 2 * TILE] + p[:, 2 * TILE :]
            terms.append(p[:GROUP] + p[GROUP:])
        for j in range(LIVE):
            acc = terms[j]
            for i in range(j):
                acc = acc + same[j, i] * terms[i]
            at = source_of[j]
            state[j, 0, shots_of(g), :] = acc[:, :TILE] + state[at, 0, shots_of(g), :]
            state[j, 1, shots_of(g), :] = acc[:, TILE:] + state[at, 1, shots_of(g), :]

        @pl.when(k < SWEEPS - 1)
        def _():
            for q in (1, 2, 4, 5):
                direction, kind = q // 3, q % 3

                @pl.when(links[q][0])
                def _(q=q, direction=direction, kind=kind):
                    first = 0 if kind == 1 else TILES_DEV - BAND
                    for e in range(BAND):
                        found = where_is[direction * TILES_DEV + first + e]
                        send[k + 1, g, direction * 16 + 4 + 4 * kind + e] = state[found, :, shots_of(g), :]
                    message(k + 1, g, q).start()

            pack_own(k + 1, g, lambda tile: where_is[tile])

        @pl.when(k == SWEEPS - 1)
        def _():
            for r in range(2 * TILES_DEV):
                final[r, :, shots_of(g), :] = state[where_is[r], :, shots_of(g), :]

    @pl.loop(0, SWEEPS * groups)
    def _(i):
        step(i // groups, i % groups)

    out_copies = []
    for r in range(2 * TILES_DEV):
        copy = pltpu.make_async_copy(
            final.at[r],
            out_hbm.at[r // TILES_DEV, :, :, pl.ds(r % TILES_DEV * TILE, TILE)],
            out_sem.at[r],
        )
        copy.start()
        out_copies.append(copy)

    @pl.loop(0, SWEEPS * groups)
    def _(i):
        for q in range(6):

            @pl.when(links[q][0])
            def _(q=q):
                message(i // groups, i % groups, q).wait_send()

    for copy in out_copies:
        copy.wait()


def body(layers, tile_devs, sources, green, rowcol, counts):
    shots, width = sources.shape[3], sources.shape[4]
    groups = shots // GROUP
    slots = green.shape[1]
    meta = jnp.concatenate([rowcol.reshape(-1), counts.reshape(-1)])
    meta = jnp.pad(meta, (0, 128 - meta.shape[0]))
    any_space = pl.BlockSpec(memory_space=pl.ANY)
    out = pl.pallas_call(
        functools.partial(kernel, layers, tile_devs, groups),
        out_shape=jax.ShapeDtypeStruct((2, 2, shots, width), F32),
        in_specs=[pl.BlockSpec(memory_space=pltpu.SMEM), any_space, any_space],
        out_specs=any_space,
        scratch_shapes=[
            pltpu.VMEM((LIVE + 2 * TILES_DEV, 2, shots, TILE), F32),
            pltpu.VMEM((SWEEPS, groups, 32, 2, GROUP, TILE), F32),
            pltpu.VMEM((SWEEPS, groups, 32, 2, GROUP, TILE), F32),
            pltpu.VMEM((32, 2, GROUP, TILE), F32),
            pltpu.VMEM((LIVE, 4 * TILE, 2 * TILE), BF16),
            pltpu.VMEM((slots, 2, TILE, TILE), F32),
            pltpu.VMEM((2 * TILES_DEV, 2, shots, TILE), F32),
            pltpu.SMEM((128,), jnp.int32),
            pltpu.SMEM((128,), jnp.int32),
            pltpu.SMEM((LIVE,), jnp.int32),
            pltpu.SMEM((LIVE,), jnp.int32),
            pltpu.SMEM((LIVE,), jnp.int32),
            pltpu.SMEM((LIVE, LIVE), F32),
            pltpu.SMEM((2 * TILES_DEV,), jnp.int32),
            pltpu.SMEM((32,), jnp.int32),
            pltpu.SemaphoreType.DMA((2 * TILES_DEV + 1,)),
            pltpu.SemaphoreType.DMA((2 * TILES_DEV,)),
            pltpu.SemaphoreType.DMA((2,)),
            pltpu.SemaphoreType.DMA((2,)),
            pltpu.SemaphoreType.DMA((SWEEPS, groups, 6)),
            pltpu.SemaphoreType.DMA((SWEEPS, groups, 6)),
        ],
        compiler_params=pltpu.CompilerParams(collective_id=0, has_side_effects=True),
    )(meta, sources[0], green[0])
    return out[None]


def solution(mesh):
    return jax.shard_map(
        functools.partial(body, mesh.shape["layer"], mesh.shape["tile"]),
        mesh=mesh,
        in_specs=(
            P("layer", None, None, None, "tile"),
            P("layer", "tile", None, None, None),
            P("layer", "tile", None),
            P("layer", "tile"),
        ),
        out_specs=P("layer", None, None, None, "tile"),
        check_vma=False,
    )
```

```python
import functools

import jax
import jax.numpy as jnp
from jax import lax
from jax.experimental import pallas as pl
from jax.experimental.pallas import tpu as pltpu
from jax.sharding import PartitionSpec as P

TILE = 128
CAP = 5
BAND = 4
SWEEPS = 5
TILES_DEV = 16
LIVE = 10
OWN = (8, 7)
GROUP = 8
SRC = LIVE
MESH = pl.DeviceIdType.MESH
VMEM = 24 << 20
F32 = jnp.float32
BF16 = jnp.bfloat16


def reader_columns(rowcol, counts, first_kind, second_kind, count):
    first = counts[first_kind]
    columns = []
    for e in range(count):
        slot_first = first_kind * CAP + min(e, CAP - 1)
        slot_second = second_kind * CAP + jnp.clip(e - first, 0, CAP - 1)
        columns.append(rowcol[1, jnp.where(e < first, slot_first, slot_second)])
    return columns


def kernel(
    layers,
    tile_devs,
    groups,
    rowcol_hbm,
    counts_hbm,
    src_hbm,
    green_hbm,
    out,
    state,
    recv,
    send,
    stage,
    weights,
    green,
    rowcol,
    counts,
    cols_next,
    counts_next,
    cols_prev,
    counts_prev,
    slot_of,
    entry_of,
    source_of,
    same,
    where_is,
    pack_of,
    local_sem,
    meta_send_sem,
    meta_recv_sem,
    send_sem,
    recv_sem,
):
    layer = lax.axis_index("layer")
    place = lax.axis_index("tile")
    up_ok, down_ok = layer > 0, layer < layers - 1
    low_ok, high_ok = place > 0, place < tile_devs - 1

    lower, upper = layer + 1, layer - 1
    links = [
        (down_ok, (lower, place), up_ok),
        (down_ok & low_ok, (lower, place - 1), up_ok & high_ok),
        (down_ok & high_ok, (lower, place + 1), up_ok & low_ok),
        (up_ok, (upper, place), down_ok),
        (up_ok & low_ok, (upper, place - 1), down_ok & high_ok),
        (up_ok & high_ok, (upper, place + 1), down_ok & low_ok),
    ]

    barrier = pltpu.get_barrier_semaphore()
    for ok, device, _ in links:

        @pl.when(ok)
        def _(device=device):
            pl.semaphore_signal(barrier, inc=1, device_id=device, device_id_type=MESH)

    list_copies = [
        pltpu.make_async_copy(there, here, local_sem.at[2 * TILES_DEV + 1 + i])
        for i, (there, here) in enumerate(((rowcol_hbm, rowcol), (counts_hbm, counts)))
    ]
    for copy in list_copies:
        copy.start()
    src_copies = []
    for direction in range(2):
        for tile in range(TILES_DEV):
            copy = pltpu.make_async_copy(
                src_hbm.at[direction, :, :, pl.ds(tile * TILE, TILE)],
                state.at[SRC + direction * TILES_DEV + tile],
                local_sem.at[direction * TILES_DEV + tile],
            )
            copy.start()
            src_copies.append(copy)
    green_copy = pltpu.make_async_copy(green_hbm, green, local_sem.at[2 * TILES_DEV])
    green_copy.start()

    @pl.when(layer == 0)
    def _():
        @pl.loop(0, SWEEPS * groups)
        def _(i):
            recv[i // groups, i % groups, pl.ds(0, 16)] = jnp.zeros((16, 2, GROUP, TILE), F32)

    @pl.when(layer == layers - 1)
    def _():
        @pl.loop(0, SWEEPS * groups)
        def _(i):
            recv[i // groups, i % groups, pl.ds(16, 16)] = jnp.zeros((16, 2, GROUP, TILE), F32)

    sides = 1 + low_ok.astype(jnp.int32) + high_ok.astype(jnp.int32)
    ends = up_ok.astype(jnp.int32) + down_ok.astype(jnp.int32)
    for copy in list_copies:
        copy.wait()
    pl.semaphore_wait(barrier, sides * ends)

    def slot_lists(side, device):
        there = ((cols_next, counts_next), (cols_prev, counts_prev))[side]
        return [
            pltpu.make_async_remote_copy(
                here,
                there[i],
                meta_send_sem.at[side, i],
                meta_recv_sem.at[side, i],
                device_id=(device, place),
                device_id_type=MESH,
            )
            for i, here in enumerate((rowcol, counts))
        ]

    @pl.when(up_ok)
    def _():
        for copy in slot_lists(0, upper):
            copy.start()

    @pl.when(down_ok)
    def _():
        for copy in slot_lists(1, lower):
            copy.start()

    def message(k, g, q):
        direction, kind = q // 3, q % 3
        base = direction * 16
        count = OWN[direction] if kind == 0 else BAND
        if kind == 0:
            source = send.at[k, g, pl.ds(base, count)]
            target = base
        elif kind == 1:
            source = send.at[k, g, pl.ds(base + 8, count)]
            target = base + 12
        else:
            source = send.at[k, g, pl.ds(base + 12, count)]
            target = base + 8
        return pltpu.make_async_remote_copy(
            source,
            recv.at[k, g, pl.ds(target, count)],
            send_sem.at[k, g, q],
            recv_sem.at[k, g, q],
            device_id=links[q][1],
            device_id_type=MESH,
        )

    def first_halo(g, q):
        direction, kind = q // 3, q % 3
        base = direction * 16
        tile = SRC + base + (0 if kind == 1 else TILES_DEV - BAND)
        target = base + (12 if kind == 1 else 8)
        return pltpu.make_async_remote_copy(
            state.at[pl.ds(tile, BAND), :, pl.ds(pl.multiple_of(g * GROUP, GROUP), GROUP), :],
            recv.at[0, g, pl.ds(target, BAND)],
            send_sem.at[0, g, q],
            recv_sem.at[0, g, q],
            device_id=links[q][1],
            device_id_type=MESH,
        )

    for copy in src_copies:
        copy.wait()
    for g in range(groups):
        for q in (1, 2, 4, 5):

            @pl.when(links[q][0])
            def _(g=g, q=q):
                first_halo(g, q).start()

    c0, c1, c2, c3 = [counts[k] for k in range(4)]
    p1, p2, p3 = c0, c0 + c1, c0 + c1 + c2
    total = p3 + c3
    targets, lives = [], []
    for j in range(LIVE):
        in1, in2, in3 = j >= p1, j >= p2, j >= p3
        kind = in1.astype(jnp.int32) + in2.astype(jnp.int32) + in3.astype(jnp.int32)
        base = jnp.where(in3, p3, jnp.where(in2, p2, jnp.where(in1, p1, 0)))
        live = j < total
        slot = jnp.where(live, kind * CAP + j - base, 0)
        row = rowcol[0, slot] - place * TILES_DEV
        col = rowcol[1, slot] - place * TILES_DEV
        reads_up = in1 & jnp.logical_not(in3)
        own = j - base + jnp.where(in3, c0, jnp.where(in2, c1, 0))
        entry = jnp.where(col < 0, 8 + BAND + col, jnp.where(col >= TILES_DEV, 12 + col - TILES_DEV, own))
        entry = entry + jnp.where(reads_up, 16, 0)
        target = row + jnp.where(in2, TILES_DEV, 0)
        slot_of[j] = slot
        entry_of[j] = jnp.where(live, entry, 0)
        source_of[j] = SRC + jnp.where(live, target, 0)
        targets.append(jnp.where(live, target, 64 + j))
        lives.append(live)
    for j in range(LIVE):
        same[j, j] = jnp.where(lives[j], 1.0, 0.0)
        for i in range(j):
            same[j, i] = jnp.where(targets[j] == targets[i], 1.0, 0.0)
    for r in range(2 * TILES_DEV):
        found = SRC + r
        for j in range(LIVE):
            found = jnp.where(targets[j] == r, j, found)
        where_is[r] = found

    @pl.when(up_ok)
    def _():
        for copy in slot_lists(0, upper):
            copy.wait_send()
        for copy in slot_lists(1, upper):
            copy.wait_recv()
        for e, column in enumerate(reader_columns(cols_prev, counts_prev, 1, 2, OWN[1])):
            pack_of[16 + e] = TILES_DEV + jnp.clip(column - place * TILES_DEV, 0, TILES_DEV - 1)

    @pl.when(down_ok)
    def _():
        for copy in slot_lists(1, lower):
            copy.wait_send()
        for copy in slot_lists(0, lower):
            copy.wait_recv()
        for e, column in enumerate(reader_columns(cols_next, counts_next, 0, 3, OWN[0])):
            pack_of[e] = jnp.clip(column - place * TILES_DEV, 0, TILES_DEV - 1)

    def shots_of(g):
        return pl.ds(pl.multiple_of(g * GROUP, GROUP), GROUP)

    def pack_own(k, g, index_of):
        for direction, ok in ((0, down_ok), (1, up_ok)):

            @pl.when(ok)
            def _(direction=direction):
                for e in range(OWN[direction]):
                    i = direction * 16 + e
                    send[k, g, i] = state[index_of(pack_of[i]), :, shots_of(g), :]
                message(k, g, direction * 3).start()

    @pl.loop(0, groups)
    def _(g):
        pack_own(0, g, lambda tile: SRC + tile)

    green_copy.wait()

    @pl.loop(0, LIVE)
    def _(j):
        blocks = green[slot_of[j]] * jnp.where(j < total, 1.0, 0.0)
        re, im = blocks[0], blocks[1]
        for row, part in enumerate((re, im)):
            high = part.astype(BF16)
            weights[j, pl.ds(row * TILE, TILE)] = high
            weights[j, pl.ds((2 + row) * TILE, TILE)] = (part - high.astype(F32)).astype(BF16)

    def step(k, g):
        for q in range(6):

            @pl.when(links[q][2])
            def _(q=q):
                message(k, g, q).wait_recv()

        stage[...] = recv[k, g]
        terms = []
        for j in range(LIVE):
            x = stage[entry_of[j]]
            x = x.reshape(2 * GROUP, TILE)
            high = x.astype(BF16)
            both = jnp.concatenate([high, (x - high.astype(F32)).astype(BF16)], axis=0)
            p = lax.dot_general(both, weights[j], (((1,), (1,)), ((), ())), preferred_element_type=F32)
            p = p[:, : 2 * TILE] + p[:, 2 * TILE :]
            p = p[: 2 * GROUP] + p[2 * GROUP :]
            by_re, by_im = p[:, :TILE], p[:, TILE:]
            terms.append((by_re[:GROUP] - by_im[GROUP:], by_im[:GROUP] + by_re[GROUP:]))
        for j in range(LIVE):
            at = source_of[j]
            for part in range(2):
                acc = terms[j][part] + state[at, part, shots_of(g), :]
                for i in range(j):
                    acc = acc + same[j, i] * terms[i][part]
                state[j, part, shots_of(g), :] = acc

        @pl.when(k < SWEEPS - 1)
        def _():
            for q in (1, 2, 4, 5):
                direction, kind = q // 3, q % 3

                @pl.when(links[q][0])
                def _(q=q, direction=direction, kind=kind):
                    first = 0 if kind == 1 else TILES_DEV - BAND
                    for e in range(BAND):
                        found = where_is[direction * TILES_DEV + first + e]
                        send[k + 1, g, direction * 16 + 4 + 4 * kind + e] = state[found, :, shots_of(g), :]
                    message(k + 1, g, q).start()

            pack_own(k + 1, g, lambda tile: where_is[tile])

        @pl.when(k == SWEEPS - 1)
        def _():
            for r in range(2 * TILES_DEV):
                columns = pl.ds(r % TILES_DEV * TILE, TILE)
                out[r // TILES_DEV, :, shots_of(g), columns] = state[where_is[r], :, shots_of(g), :]

    @pl.loop(0, SWEEPS * groups)
    def _(i):
        step(i // groups, i % groups)

    @pl.loop(0, SWEEPS * groups)
    def _(i):
        for q in range(6):

            @pl.when(links[q][0])
            def _(q=q):
                message(i // groups, i % groups, q).wait_send()


def put_out(there, out, sem):
    copy = pltpu.make_async_copy(there, out, sem)
    copy.start()
    copy.wait()


def body(layers, tile_devs, sources, green, rowcol, counts):
    shots, width = sources.shape[3], sources.shape[4]
    groups = shots // GROUP
    slots = green.shape[1]
    in_hbm = pl.BlockSpec(memory_space=pltpu.HBM)
    traces = pl.pallas_call(
        functools.partial(kernel, layers, tile_devs, groups),
        out_shape=jax.ShapeDtypeStruct((2, 2, shots, width), F32),
        in_specs=[in_hbm] * 4,
        out_specs=pl.BlockSpec(memory_space=pltpu.VMEM),
        scratch_shapes=[
            pltpu.VMEM((LIVE + 2 * TILES_DEV, 2, shots, TILE), F32),
            pltpu.VMEM((SWEEPS, groups, 32, 2, GROUP, TILE), F32),
            pltpu.VMEM((SWEEPS, groups, 32, 2, GROUP, TILE), F32),
            pltpu.VMEM((32, 2, GROUP, TILE), F32),
            pltpu.VMEM((LIVE, 4 * TILE, TILE), BF16),
            pltpu.VMEM((slots, 2, TILE, TILE), F32),
            pltpu.SMEM((2, slots), jnp.int32),
            pltpu.SMEM((4,), jnp.int32),
            pltpu.SMEM((2, slots), jnp.int32),
            pltpu.SMEM((4,), jnp.int32),
            pltpu.SMEM((2, slots), jnp.int32),
            pltpu.SMEM((4,), jnp.int32),
            pltpu.SMEM((LIVE,), jnp.int32),
            pltpu.SMEM((LIVE,), jnp.int32),
            pltpu.SMEM((LIVE,), jnp.int32),
            pltpu.SMEM((LIVE, LIVE), F32),
            pltpu.SMEM((2 * TILES_DEV,), jnp.int32),
            pltpu.SMEM((32,), jnp.int32),
            pltpu.SemaphoreType.DMA((2 * TILES_DEV + 3,)),
            pltpu.SemaphoreType.DMA((2, 2)),
            pltpu.SemaphoreType.DMA((2, 2)),
            pltpu.SemaphoreType.DMA((SWEEPS, groups, 6)),
            pltpu.SemaphoreType.DMA((SWEEPS, groups, 6)),
        ],
        compiler_params=pltpu.CompilerParams(collective_id=0, has_side_effects=True, vmem_limit_bytes=VMEM),
    )(*[pltpu.with_memory_space_constraint(x, pltpu.HBM) for x in (rowcol[0].T, counts[0], sources[0], green[0])])
    out = pl.pallas_call(
        put_out,
        out_shape=jax.ShapeDtypeStruct((2, 2, shots, width), F32),
        in_specs=[pl.BlockSpec(memory_space=pltpu.VMEM)],
        out_specs=in_hbm,
        scratch_shapes=[pltpu.SemaphoreType.DMA],
        compiler_params=pltpu.CompilerParams(vmem_limit_bytes=4 << 20),
    )(traces)
    return out[None]


def solution(mesh):
    return jax.shard_map(
        functools.partial(body, mesh.shape["layer"], mesh.shape["tile"]),
        mesh=mesh,
        in_specs=(
            P("layer", None, None, None, "tile"),
            P("layer", "tile", None, None, None),
            P("layer", "tile", None),
            P("layer", "tile"),
        ),
        out_specs=P("layer", None, None, None, "tile"),
        check_vma=False,
    )
```

```python
import functools

import jax
import jax.numpy as jnp
from jax import lax
from jax.experimental import pallas as pl
from jax.experimental.pallas import tpu as pltpu
from jax.sharding import PartitionSpec as P

TILE = 128
CAP = 5
BAND = 4
SWEEPS = 5
TILES_DEV = 16
LIVE = 10
OWN = (8, 7)
GROUP = 8
SRC = LIVE
MESH = pl.DeviceIdType.MESH
VMEM = 24 << 20
F32 = jnp.float32
BF16 = jnp.bfloat16


def reader_columns(rowcol, counts, first_kind, second_kind, count):
    first = counts[first_kind]
    columns = []
    for e in range(count):
        slot_first = first_kind * CAP + min(e, CAP - 1)
        slot_second = second_kind * CAP + jnp.clip(e - first, 0, CAP - 1)
        columns.append(rowcol[1, jnp.where(e < first, slot_first, slot_second)])
    return columns


def kernel(
    layers,
    tile_devs,
    groups,
    rowcol_hbm,
    counts_hbm,
    src_hbm,
    green_hbm,
    out,
    state,
    recv,
    recv_whole,
    send,
    stage,
    weights,
    green,
    rowcol,
    counts,
    cols_next,
    counts_next,
    cols_prev,
    counts_prev,
    slot_of,
    entry_of,
    source_of,
    same,
    where_is,
    pack_of,
    local_sem,
    meta_send_sem,
    meta_recv_sem,
    send_sem,
    recv_sem,
):
    layer = lax.axis_index("layer")
    place = lax.axis_index("tile")
    up_ok, down_ok = layer > 0, layer < layers - 1
    low_ok, high_ok = place > 0, place < tile_devs - 1

    lower, upper = layer + 1, layer - 1
    links = [
        (down_ok, (lower, place), up_ok),
        (down_ok & low_ok, (lower, place - 1), up_ok & high_ok),
        (down_ok & high_ok, (lower, place + 1), up_ok & low_ok),
        (up_ok, (upper, place), down_ok),
        (up_ok & low_ok, (upper, place - 1), down_ok & high_ok),
        (up_ok & high_ok, (upper, place + 1), down_ok & low_ok),
    ]

    barrier = pltpu.get_barrier_semaphore()
    for ok, device, _ in links:

        @pl.when(ok)
        def _(device=device):
            pl.semaphore_signal(barrier, inc=1, device_id=device, device_id_type=MESH)

    list_copies = [
        pltpu.make_async_copy(there, here, local_sem.at[2 * TILES_DEV + 1 + i])
        for i, (there, here) in enumerate(((rowcol_hbm, rowcol), (counts_hbm, counts)))
    ]
    for copy in list_copies:
        copy.start()
    src_copies = []
    for direction in range(2):
        for tile in range(TILES_DEV):
            copy = pltpu.make_async_copy(
                src_hbm.at[direction, :, :, pl.ds(tile * TILE, TILE)],
                state.at[SRC + direction * TILES_DEV + tile],
                local_sem.at[direction * TILES_DEV + tile],
            )
            copy.start()
            src_copies.append(copy)
    green_copy = pltpu.make_async_copy(green_hbm, green, local_sem.at[2 * TILES_DEV])
    green_copy.start()

    @pl.when(layer == 0)
    def _():
        recv_whole[0] = jnp.zeros((TILES_DEV, 2, GROUP, TILE), F32)

        @pl.loop(0, SWEEPS * groups)
        def _(i):
            recv[i // groups, i % groups, pl.ds(0, 16)] = jnp.zeros((16, 2, GROUP, TILE), F32)

    @pl.when(layer == layers - 1)
    def _():
        recv_whole[1] = jnp.zeros((TILES_DEV, 2, GROUP, TILE), F32)

        @pl.loop(0, SWEEPS * groups)
        def _(i):
            recv[i // groups, i % groups, pl.ds(16, 16)] = jnp.zeros((16, 2, GROUP, TILE), F32)

    sides = 1 + low_ok.astype(jnp.int32) + high_ok.astype(jnp.int32)
    ends = up_ok.astype(jnp.int32) + down_ok.astype(jnp.int32)
    for copy in list_copies:
        copy.wait()
    pl.semaphore_wait(barrier, sides * ends)

    def slot_lists(side, device):
        there = ((cols_next, counts_next), (cols_prev, counts_prev))[side]
        return [
            pltpu.make_async_remote_copy(
                here,
                there[i],
                meta_send_sem.at[side, i],
                meta_recv_sem.at[side, i],
                device_id=(device, place),
                device_id_type=MESH,
            )
            for i, here in enumerate((rowcol, counts))
        ]

    @pl.when(up_ok)
    def _():
        for copy in slot_lists(0, upper):
            copy.start()

    @pl.when(down_ok)
    def _():
        for copy in slot_lists(1, lower):
            copy.start()

    def message(k, g, q):
        direction, kind = q // 3, q % 3
        base = direction * 16
        count = OWN[direction] if kind == 0 else BAND
        if kind == 0:
            source = send.at[k, g, pl.ds(base, count)]
            target = base
        elif kind == 1:
            source = send.at[k, g, pl.ds(base + 8, count)]
            target = base + 12
        else:
            source = send.at[k, g, pl.ds(base + 12, count)]
            target = base + 8
        return pltpu.make_async_remote_copy(
            source,
            recv.at[k, g, pl.ds(target, count)],
            send_sem.at[k, g, q],
            recv_sem.at[k, g, q],
            device_id=links[q][1],
            device_id_type=MESH,
        )

    def first_halo(g, q):
        direction, kind = q // 3, q % 3
        base = direction * 16
        tile = SRC + base + (0 if kind == 1 else TILES_DEV - BAND)
        target = base + (12 if kind == 1 else 8)
        return pltpu.make_async_remote_copy(
            state.at[pl.ds(tile, BAND), :, pl.ds(pl.multiple_of(g * GROUP, GROUP), GROUP), :],
            recv.at[0, g, pl.ds(target, BAND)],
            send_sem.at[0, g, q],
            recv_sem.at[0, g, q],
            device_id=links[q][1],
            device_id_type=MESH,
        )

    for copy in src_copies:
        copy.wait()
    def first_own(direction):
        q = 3 * direction
        return pltpu.make_async_remote_copy(
            state.at[pl.ds(SRC + direction * TILES_DEV, TILES_DEV), :, pl.ds(0, GROUP), :],
            recv_whole.at[direction],
            send_sem.at[0, 0, q],
            recv_sem.at[0, 0, q],
            device_id=links[q][1],
            device_id_type=MESH,
        )

    for g in range(groups):
        for q in (1, 2, 4, 5):

            @pl.when(links[q][0])
            def _(g=g, q=q):
                first_halo(g, q).start()

        if g == 0:
            for direction in range(2):

                @pl.when(links[3 * direction][0])
                def _(direction=direction):
                    first_own(direction).start()

    c0, c1, c2, c3 = [counts[k] for k in range(4)]
    p1, p2, p3 = c0, c0 + c1, c0 + c1 + c2
    total = p3 + c3
    targets, lives = [], []
    for j in range(LIVE):
        in1, in2, in3 = j >= p1, j >= p2, j >= p3
        kind = in1.astype(jnp.int32) + in2.astype(jnp.int32) + in3.astype(jnp.int32)
        base = jnp.where(in3, p3, jnp.where(in2, p2, jnp.where(in1, p1, 0)))
        live = j < total
        slot = jnp.where(live, kind * CAP + j - base, 0)
        row = rowcol[0, slot] - place * TILES_DEV
        col = rowcol[1, slot] - place * TILES_DEV
        reads_up = in1 & jnp.logical_not(in3)
        own = j - base + jnp.where(in3, c0, jnp.where(in2, c1, 0))
        half = jnp.where(reads_up, 16, 0)
        halo = jnp.where(col < 0, 8 + BAND + col, 12 + col - TILES_DEV)
        inside = (col >= 0) & (col < TILES_DEV)
        target = row + jnp.where(in2, TILES_DEV, 0)
        slot_of[j] = slot
        entry_of[0, j] = jnp.where(live, half + jnp.where(inside, own, halo), 0)
        entry_of[1, j] = jnp.where(live, half + jnp.where(inside, 32 + col, halo), 32)
        source_of[j] = SRC + jnp.where(live, target, 0)
        targets.append(jnp.where(live, target, 64 + j))
        lives.append(live)
    for j in range(LIVE):
        same[j, j] = jnp.where(lives[j], 1.0, 0.0)
        for i in range(j):
            same[j, i] = jnp.where(targets[j] == targets[i], 1.0, 0.0)
    for r in range(2 * TILES_DEV):
        found = SRC + r
        for j in range(LIVE):
            found = jnp.where(targets[j] == r, j, found)
        where_is[r] = found

    @pl.when(up_ok)
    def _():
        for copy in slot_lists(0, upper):
            copy.wait_send()
        for copy in slot_lists(1, upper):
            copy.wait_recv()
        for e, column in enumerate(reader_columns(cols_prev, counts_prev, 1, 2, OWN[1])):
            pack_of[16 + e] = TILES_DEV + jnp.clip(column - place * TILES_DEV, 0, TILES_DEV - 1)

    @pl.when(down_ok)
    def _():
        for copy in slot_lists(1, lower):
            copy.wait_send()
        for copy in slot_lists(0, lower):
            copy.wait_recv()
        for e, column in enumerate(reader_columns(cols_next, counts_next, 0, 3, OWN[0])):
            pack_of[e] = jnp.clip(column - place * TILES_DEV, 0, TILES_DEV - 1)

    def shots_of(g):
        return pl.ds(pl.multiple_of(g * GROUP, GROUP), GROUP)

    def pack_own(k, g, index_of):
        for direction, ok in ((0, down_ok), (1, up_ok)):

            @pl.when(ok)
            def _(direction=direction):
                for e in range(OWN[direction]):
                    i = direction * 16 + e
                    send[k, g, i] = state[index_of(pack_of[i]), :, shots_of(g), :]
                message(k, g, direction * 3).start()

    @pl.loop(1, groups)
    def _(g):
        pack_own(0, g, lambda tile: SRC + tile)

    green_copy.wait()

    @pl.loop(0, LIVE)
    def _(j):
        blocks = green[slot_of[j]] * jnp.where(j < total, 1.0, 0.0)
        re, im = blocks[0], blocks[1]
        for column, part in enumerate((re.T, im.T)):
            high = part.astype(BF16)
            weights[j, :, pl.ds(column * TILE, TILE)] = high
            weights[j, :, pl.ds((2 + column) * TILE, TILE)] = (part - high.astype(F32)).astype(BF16)

    for direction in range(2):

        @pl.when(links[3 * direction][2])
        def _(direction=direction):
            first_own(direction).wait_recv()

        stage[pl.ds(32 + direction * TILES_DEV, TILES_DEV)] = recv_whole[direction]

    def step(k, g):
        later = (k > 0) | (g > 0)
        whole = jnp.where(later, 0, 1)
        for q in range(6):

            @pl.when(links[q][2] & (later if q % 3 == 0 else True))
            def _(q=q):
                message(k, g, q).wait_recv()

        stage[pl.ds(0, 32)] = recv[k, g]
        terms = []
        for j in range(LIVE):
            x = stage[entry_of[whole, j]]
            x = x.reshape(2 * GROUP, TILE)
            high = x.astype(BF16)
            both = jnp.concatenate([high, (x - high.astype(F32)).astype(BF16)], axis=0)
            p = lax.dot_general(both, weights[j], (((1,), (0,)), ((), ())), preferred_element_type=F32)
            p = p[:, : 2 * TILE] + p[:, 2 * TILE :]
            p = p[: 2 * GROUP] + p[2 * GROUP :]
            by_re, by_im = p[:, :TILE], p[:, TILE:]
            terms.append((by_re[:GROUP] - by_im[GROUP:], by_im[:GROUP] + by_re[GROUP:]))
        for j in range(LIVE):
            at = source_of[j]
            for part in range(2):
                acc = terms[j][part] + state[at, part, shots_of(g), :]
                for i in range(j):
                    acc = acc + same[j, i] * terms[i][part]
                state[j, part, shots_of(g), :] = acc

        @pl.when(k < SWEEPS - 1)
        def _():
            for q in (1, 2, 4, 5):
                direction, kind = q // 3, q % 3

                @pl.when(links[q][0])
                def _(q=q, direction=direction, kind=kind):
                    first = 0 if kind == 1 else TILES_DEV - BAND
                    for e in range(BAND):
                        found = where_is[direction * TILES_DEV + first + e]
                        send[k + 1, g, direction * 16 + 4 + 4 * kind + e] = state[found, :, shots_of(g), :]
                    message(k + 1, g, q).start()

            pack_own(k + 1, g, lambda tile: where_is[tile])

        @pl.when(k == SWEEPS - 1)
        def _():
            for r in range(2 * TILES_DEV):
                columns = pl.ds(r % TILES_DEV * TILE, TILE)
                out[r // TILES_DEV, :, shots_of(g), columns] = state[where_is[r], :, shots_of(g), :]

    @pl.loop(0, SWEEPS * groups)
    def _(i):
        step(i // groups, i % groups)

    for direction in range(2):

        @pl.when(links[3 * direction][0])
        def _(direction=direction):
            first_own(direction).wait_send()

    @pl.loop(0, SWEEPS * groups)
    def _(i):
        for q in range(6):

            @pl.when(links[q][0] & ((i > 0) if q % 3 == 0 else True))
            def _(q=q):
                message(i // groups, i % groups, q).wait_send()


def put_out(there, out, sem):
    copy = pltpu.make_async_copy(there, out, sem)
    copy.start()
    copy.wait()


def body(layers, tile_devs, sources, green, rowcol, counts):
    shots, width = sources.shape[3], sources.shape[4]
    groups = shots // GROUP
    slots = green.shape[1]
    in_hbm = pl.BlockSpec(memory_space=pltpu.HBM)
    traces = pl.pallas_call(
        functools.partial(kernel, layers, tile_devs, groups),
        out_shape=jax.ShapeDtypeStruct((2, 2, shots, width), F32),
        in_specs=[in_hbm] * 4,
        out_specs=pl.BlockSpec(memory_space=pltpu.VMEM),
        scratch_shapes=[
            pltpu.VMEM((LIVE + 2 * TILES_DEV, 2, shots, TILE), F32),
            pltpu.VMEM((SWEEPS, groups, 32, 2, GROUP, TILE), F32),
            pltpu.VMEM((2, TILES_DEV, 2, GROUP, TILE), F32),
            pltpu.VMEM((SWEEPS, groups, 32, 2, GROUP, TILE), F32),
            pltpu.VMEM((64, 2, GROUP, TILE), F32),
            pltpu.VMEM((LIVE, TILE, 4 * TILE), BF16),
            pltpu.VMEM((slots, 2, TILE, TILE), F32),
            pltpu.SMEM((2, slots), jnp.int32),
            pltpu.SMEM((4,), jnp.int32),
            pltpu.SMEM((2, slots), jnp.int32),
            pltpu.SMEM((4,), jnp.int32),
            pltpu.SMEM((2, slots), jnp.int32),
            pltpu.SMEM((4,), jnp.int32),
            pltpu.SMEM((LIVE,), jnp.int32),
            pltpu.SMEM((2, LIVE), jnp.int32),
            pltpu.SMEM((LIVE,), jnp.int32),
            pltpu.SMEM((LIVE, LIVE), F32),
            pltpu.SMEM((2 * TILES_DEV,), jnp.int32),
            pltpu.SMEM((32,), jnp.int32),
            pltpu.SemaphoreType.DMA((2 * TILES_DEV + 3,)),
            pltpu.SemaphoreType.DMA((2, 2)),
            pltpu.SemaphoreType.DMA((2, 2)),
            pltpu.SemaphoreType.DMA((SWEEPS, groups, 6)),
            pltpu.SemaphoreType.DMA((SWEEPS, groups, 6)),
        ],
        compiler_params=pltpu.CompilerParams(collective_id=0, has_side_effects=True, vmem_limit_bytes=VMEM),
    )(*[pltpu.with_memory_space_constraint(x, pltpu.HBM) for x in (rowcol[0].T, counts[0], sources[0], green[0])])
    out = pl.pallas_call(
        put_out,
        out_shape=jax.ShapeDtypeStruct((2, 2, shots, width), F32),
        in_specs=[pl.BlockSpec(memory_space=pltpu.VMEM)],
        out_specs=in_hbm,
        scratch_shapes=[pltpu.SemaphoreType.DMA],
        compiler_params=pltpu.CompilerParams(vmem_limit_bytes=4 << 20),
    )(traces)
    return out[None]


def solution(mesh):
    return jax.shard_map(
        functools.partial(body, mesh.shape["layer"], mesh.shape["tile"]),
        mesh=mesh,
        in_specs=(
            P("layer", None, None, None, "tile"),
            P("layer", "tile", None, None, None),
            P("layer", "tile", None),
            P("layer", "tile"),
        ),
        out_specs=P("layer", None, None, None, "tile"),
        check_vma=False,
    )
```

```python
import functools

import jax
import jax.numpy as jnp
from jax import lax
from jax.experimental import pallas as pl
from jax.experimental.pallas import tpu as pltpu
from jax.sharding import PartitionSpec as P

TILE = 128
CAP = 5
BAND = 4
SWEEPS = 5
TILES_DEV = 16
LIVE = 10
OWN = (8, 7)
GROUP = 8
SRC = LIVE
MESH = pl.DeviceIdType.MESH
VMEM = 24 << 20
F32 = jnp.float32
BF16 = jnp.bfloat16


def reader_columns(rowcol, counts, first_kind, second_kind, count):
    first = counts[first_kind]
    columns = []
    for e in range(count):
        slot_first = first_kind * CAP + min(e, CAP - 1)
        slot_second = second_kind * CAP + jnp.clip(e - first, 0, CAP - 1)
        columns.append(rowcol[1, jnp.where(e < first, slot_first, slot_second)])
    return columns


def kernel(
    layers,
    tile_devs,
    groups,
    rowcol_hbm,
    counts_hbm,
    src_hbm,
    green_hbm,
    out,
    state,
    recv,
    recv_whole,
    send,
    stage,
    weights,
    green,
    rowcol,
    counts,
    cols_next,
    counts_next,
    cols_prev,
    counts_prev,
    slot_of,
    entry_of,
    source_of,
    same,
    where_is,
    pack_of,
    local_sem,
    meta_send_sem,
    meta_recv_sem,
    send_sem,
    recv_sem,
):
    layer = lax.axis_index("layer")
    place = lax.axis_index("tile")
    up_ok, down_ok = layer > 0, layer < layers - 1
    low_ok, high_ok = place > 0, place < tile_devs - 1

    lower, upper = layer + 1, layer - 1
    links = [
        (down_ok, (lower, place), up_ok),
        (down_ok & low_ok, (lower, place - 1), up_ok & high_ok),
        (down_ok & high_ok, (lower, place + 1), up_ok & low_ok),
        (up_ok, (upper, place), down_ok),
        (up_ok & low_ok, (upper, place - 1), down_ok & high_ok),
        (up_ok & high_ok, (upper, place + 1), down_ok & low_ok),
    ]

    barrier = pltpu.get_barrier_semaphore()
    for ok, device, _ in links:

        @pl.when(ok)
        def _(device=device):
            pl.semaphore_signal(barrier, inc=1, device_id=device, device_id_type=MESH)

    list_copies = [
        pltpu.make_async_copy(there, here, local_sem.at[2 * TILES_DEV + 1 + i])
        for i, (there, here) in enumerate(((rowcol_hbm, rowcol), (counts_hbm, counts)))
    ]
    for copy in list_copies:
        copy.start()
    src_copies = []
    for direction in range(2):
        for tile in range(TILES_DEV):
            copy = pltpu.make_async_copy(
                src_hbm.at[direction, :, :, pl.ds(tile * TILE, TILE)],
                state.at[SRC + direction * TILES_DEV + tile],
                local_sem.at[direction * TILES_DEV + tile],
            )
            copy.start()
            src_copies.append(copy)
    green_copy = pltpu.make_async_copy(green_hbm, green, local_sem.at[2 * TILES_DEV])
    green_copy.start()

    @pl.when(layer == 0)
    def _():
        recv_whole[0] = jnp.zeros((TILES_DEV, 2, GROUP, TILE), F32)

        @pl.loop(0, SWEEPS * groups)
        def _(i):
            recv[i // groups, i % groups, pl.ds(0, 16)] = jnp.zeros((16, 2, GROUP, TILE), F32)

    @pl.when(layer == layers - 1)
    def _():
        recv_whole[1] = jnp.zeros((TILES_DEV, 2, GROUP, TILE), F32)

        @pl.loop(0, SWEEPS * groups)
        def _(i):
            recv[i // groups, i % groups, pl.ds(16, 16)] = jnp.zeros((16, 2, GROUP, TILE), F32)

    sides = 1 + low_ok.astype(jnp.int32) + high_ok.astype(jnp.int32)
    ends = up_ok.astype(jnp.int32) + down_ok.astype(jnp.int32)
    for copy in list_copies:
        copy.wait()
    pl.semaphore_wait(barrier, sides * ends)

    def slot_lists(side, device):
        there = ((cols_next, counts_next), (cols_prev, counts_prev))[side]
        return [
            pltpu.make_async_remote_copy(
                here,
                there[i],
                meta_send_sem.at[side, i],
                meta_recv_sem.at[side, i],
                device_id=(device, place),
                device_id_type=MESH,
            )
            for i, here in enumerate((rowcol, counts))
        ]

    @pl.when(up_ok)
    def _():
        for copy in slot_lists(0, upper):
            copy.start()

    @pl.when(down_ok)
    def _():
        for copy in slot_lists(1, lower):
            copy.start()

    def message(k, g, q):
        direction, kind = q // 3, q % 3
        base = direction * 16
        count = OWN[direction] if kind == 0 else BAND
        if kind == 0:
            source = send.at[k, g, pl.ds(base, count)]
            target = base
        elif kind == 1:
            source = send.at[k, g, pl.ds(base + 8, count)]
            target = base + 12
        else:
            source = send.at[k, g, pl.ds(base + 12, count)]
            target = base + 8
        return pltpu.make_async_remote_copy(
            source,
            recv.at[k, g, pl.ds(target, count)],
            send_sem.at[k, g, q],
            recv_sem.at[k, g, q],
            device_id=links[q][1],
            device_id_type=MESH,
        )

    def first_halo(g, q):
        direction, kind = q // 3, q % 3
        base = direction * 16
        tile = SRC + base + (0 if kind == 1 else TILES_DEV - BAND)
        target = base + (12 if kind == 1 else 8)
        return pltpu.make_async_remote_copy(
            state.at[pl.ds(tile, BAND), :, pl.ds(pl.multiple_of(g * GROUP, GROUP), GROUP), :],
            recv.at[0, g, pl.ds(target, BAND)],
            send_sem.at[0, g, q],
            recv_sem.at[0, g, q],
            device_id=links[q][1],
            device_id_type=MESH,
        )

    for copy in src_copies:
        copy.wait()
    def first_own(direction):
        q = 3 * direction
        return pltpu.make_async_remote_copy(
            state.at[pl.ds(SRC + direction * TILES_DEV, TILES_DEV), :, pl.ds(0, GROUP), :],
            recv_whole.at[direction],
            send_sem.at[0, 0, q],
            recv_sem.at[0, 0, q],
            device_id=links[q][1],
            device_id_type=MESH,
        )

    for g in range(groups):
        for q in (1, 2, 4, 5):

            @pl.when(links[q][0])
            def _(g=g, q=q):
                first_halo(g, q).start()

        if g == 0:
            for direction in range(2):

                @pl.when(links[3 * direction][0])
                def _(direction=direction):
                    first_own(direction).start()

    c0, c1, c2, c3 = [counts[k] for k in range(4)]
    p1, p2, p3 = c0, c0 + c1, c0 + c1 + c2
    total = p3 + c3
    targets, lives = [], []
    for j in range(LIVE):
        in1, in2, in3 = j >= p1, j >= p2, j >= p3
        kind = in1.astype(jnp.int32) + in2.astype(jnp.int32) + in3.astype(jnp.int32)
        base = jnp.where(in3, p3, jnp.where(in2, p2, jnp.where(in1, p1, 0)))
        live = j < total
        slot = jnp.where(live, kind * CAP + j - base, 0)
        row = rowcol[0, slot] - place * TILES_DEV
        col = rowcol[1, slot] - place * TILES_DEV
        reads_up = in1 & jnp.logical_not(in3)
        own = j - base + jnp.where(in3, c0, jnp.where(in2, c1, 0))
        half = jnp.where(reads_up, 16, 0)
        halo = jnp.where(col < 0, 8 + BAND + col, 12 + col - TILES_DEV)
        inside = (col >= 0) & (col < TILES_DEV)
        target = row + jnp.where(in2, TILES_DEV, 0)
        slot_of[j] = slot
        entry_of[0, j] = jnp.where(live, half + jnp.where(inside, own, halo), 0)
        entry_of[1, j] = jnp.where(live, half + jnp.where(inside, 32 + col, halo), 32)
        source_of[j] = SRC + jnp.where(live, target, 0)
        targets.append(jnp.where(live, target, 64 + j))
        lives.append(live)
    for j in range(LIVE):
        same[j, j] = jnp.where(lives[j], 1.0, 0.0)
        for i in range(j):
            same[j, i] = jnp.where(targets[j] == targets[i], 1.0, 0.0)
    for r in range(2 * TILES_DEV):
        found = SRC + r
        for j in range(LIVE):
            found = jnp.where(targets[j] == r, j, found)
        where_is[r] = found

    @pl.when(up_ok)
    def _():
        for copy in slot_lists(0, upper):
            copy.wait_send()
        for copy in slot_lists(1, upper):
            copy.wait_recv()
        for e, column in enumerate(reader_columns(cols_prev, counts_prev, 1, 2, OWN[1])):
            pack_of[16 + e] = TILES_DEV + jnp.clip(column - place * TILES_DEV, 0, TILES_DEV - 1)

    @pl.when(down_ok)
    def _():
        for copy in slot_lists(1, lower):
            copy.wait_send()
        for copy in slot_lists(0, lower):
            copy.wait_recv()
        for e, column in enumerate(reader_columns(cols_next, counts_next, 0, 3, OWN[0])):
            pack_of[e] = jnp.clip(column - place * TILES_DEV, 0, TILES_DEV - 1)

    def shots_of(g):
        return pl.ds(pl.multiple_of(g * GROUP, GROUP), GROUP)

    def pack_own(k, g, index_of):
        for direction, ok in ((0, down_ok), (1, up_ok)):

            @pl.when(ok)
            def _(direction=direction):
                for e in range(OWN[direction]):
                    i = direction * 16 + e
                    send[k, g, i] = state[index_of(pack_of[i]), :, shots_of(g), :]
                message(k, g, direction * 3).start()

    @pl.loop(1, groups)
    def _(g):
        pack_own(0, g, lambda tile: SRC + tile)

    green_copy.wait()

    @pl.loop(0, LIVE)
    def _(j):
        blocks = green[slot_of[j]] * jnp.where(j < total, 1.0, 0.0)
        re, im = blocks[0], blocks[1]
        for column, part in enumerate((re.T, im.T)):
            high = part.astype(BF16)
            weights[j, :, pl.ds(column * TILE, TILE)] = high
            weights[j, :, pl.ds((2 + column) * TILE, TILE)] = (part - high.astype(F32)).astype(BF16)

    for direction in range(2):

        @pl.when(links[3 * direction][2])
        def _(direction=direction):
            first_own(direction).wait_recv()

        @pl.when(links[3 * direction][0])
        def _(direction=direction):
            first_own(direction).wait_send()

        stage[pl.ds(32 + direction * TILES_DEV, TILES_DEV)] = recv_whole[direction]

    def step(k, g):
        later = (k > 0) | (g > 0)
        whole = jnp.where(later, 0, 1)
        for q in range(6):

            @pl.when(links[q][0] & (later if q % 3 == 0 else True))
            def _(q=q):
                message(k, g, q).wait_send()

        for q in range(6):

            @pl.when(links[q][2] & (later if q % 3 == 0 else True))
            def _(q=q):
                message(k, g, q).wait_recv()

        stage[pl.ds(0, 32)] = recv[k, g]
        terms = []
        for j in range(LIVE):
            x = stage[entry_of[whole, j]]
            x = x.reshape(2 * GROUP, TILE)
            high = x.astype(BF16)
            both = jnp.concatenate([high, (x - high.astype(F32)).astype(BF16)], axis=0)
            p = lax.dot_general(both, weights[j], (((1,), (0,)), ((), ())), preferred_element_type=F32)
            p = p[:, : 2 * TILE] + p[:, 2 * TILE :]
            p = p[: 2 * GROUP] + p[2 * GROUP :]
            by_re, by_im = p[:, :TILE], p[:, TILE:]
            terms.append((by_re[:GROUP] - by_im[GROUP:], by_im[:GROUP] + by_re[GROUP:]))
        for j in range(LIVE):
            at = source_of[j]
            for part in range(2):
                acc = terms[j][part] + state[at, part, shots_of(g), :]
                for i in range(j):
                    acc = acc + same[j, i] * terms[i][part]
                state[j, part, shots_of(g), :] = acc

        @pl.when(k < SWEEPS - 1)
        def _():
            for direction, own_ok in ((0, down_ok), (1, up_ok)):
                for kind in (1, 2):
                    q = 3 * direction + kind

                    @pl.when(links[q][0])
                    def _(q=q, direction=direction, kind=kind):
                        first = 0 if kind == 1 else TILES_DEV - BAND
                        for e in range(BAND):
                            found = where_is[direction * TILES_DEV + first + e]
                            send[k + 1, g, direction * 16 + 4 + 4 * kind + e] = state[found, :, shots_of(g), :]
                        message(k + 1, g, q).start()

                @pl.when(own_ok)
                def _(direction=direction):
                    for e in range(OWN[direction]):
                        i = direction * 16 + e
                        send[k + 1, g, i] = state[where_is[pack_of[i]], :, shots_of(g), :]
                    message(k + 1, g, direction * 3).start()

        @pl.when(k == SWEEPS - 1)
        def _():
            for r in range(2 * TILES_DEV):
                columns = pl.ds(r % TILES_DEV * TILE, TILE)
                out[r // TILES_DEV, :, shots_of(g), columns] = state[where_is[r], :, shots_of(g), :]

    @pl.loop(0, SWEEPS * groups)
    def _(i):
        step(i // groups, i % groups)


def body(layers, tile_devs, sources, green, rowcol, counts):
    shots, width = sources.shape[3], sources.shape[4]
    groups = shots // GROUP
    slots = green.shape[1]
    in_hbm = pl.BlockSpec(memory_space=pltpu.HBM)
    traces = pl.pallas_call(
        functools.partial(kernel, layers, tile_devs, groups),
        out_shape=jax.ShapeDtypeStruct((2, 2, shots, width), F32),
        in_specs=[in_hbm] * 4,
        out_specs=pl.BlockSpec(memory_space=pltpu.VMEM),
        scratch_shapes=[
            pltpu.VMEM((LIVE + 2 * TILES_DEV, 2, shots, TILE), F32),
            pltpu.VMEM((SWEEPS, groups, 32, 2, GROUP, TILE), F32),
            pltpu.VMEM((2, TILES_DEV, 2, GROUP, TILE), F32),
            pltpu.VMEM((SWEEPS, groups, 32, 2, GROUP, TILE), F32),
            pltpu.VMEM((64, 2, GROUP, TILE), F32),
            pltpu.VMEM((LIVE, TILE, 4 * TILE), BF16),
            pltpu.VMEM((slots, 2, TILE, TILE), F32),
            pltpu.SMEM((2, slots), jnp.int32),
            pltpu.SMEM((4,), jnp.int32),
            pltpu.SMEM((2, slots), jnp.int32),
            pltpu.SMEM((4,), jnp.int32),
            pltpu.SMEM((2, slots), jnp.int32),
            pltpu.SMEM((4,), jnp.int32),
            pltpu.SMEM((LIVE,), jnp.int32),
            pltpu.SMEM((2, LIVE), jnp.int32),
            pltpu.SMEM((LIVE,), jnp.int32),
            pltpu.SMEM((LIVE, LIVE), F32),
            pltpu.SMEM((2 * TILES_DEV,), jnp.int32),
            pltpu.SMEM((32,), jnp.int32),
            pltpu.SemaphoreType.DMA((2 * TILES_DEV + 3,)),
            pltpu.SemaphoreType.DMA((2, 2)),
            pltpu.SemaphoreType.DMA((2, 2)),
            pltpu.SemaphoreType.DMA((SWEEPS, groups, 6)),
            pltpu.SemaphoreType.DMA((SWEEPS, groups, 6)),
        ],
        compiler_params=pltpu.CompilerParams(collective_id=0, has_side_effects=True, vmem_limit_bytes=VMEM),
    )(*[pltpu.with_memory_space_constraint(x, pltpu.HBM) for x in (rowcol[0].T, counts[0], sources[0], green[0])])
    return traces[None]


def solution(mesh):
    return jax.shard_map(
        functools.partial(body, mesh.shape["layer"], mesh.shape["tile"]),
        mesh=mesh,
        in_specs=(
            P("layer", None, None, None, "tile"),
            P("layer", "tile", None, None, None),
            P("layer", "tile", None),
            P("layer", "tile"),
        ),
        out_specs=P("layer", None, None, None, "tile"),
        check_vma=False,
    )
```

```python
import functools

import jax
import jax.numpy as jnp
from jax import lax
from jax.experimental import pallas as pl
from jax.experimental.pallas import tpu as pltpu
from jax.sharding import PartitionSpec as P

TILE = 128
CAP = 5
BAND = 4
SWEEPS = 5
TILES_DEV = 16
LIVE = 10
OWN = (8, 7)
GROUP = 8
SRC = LIVE
MESH = pl.DeviceIdType.MESH
VMEM = 24 << 20
F32 = jnp.float32
BF16 = jnp.bfloat16


def reader_columns(rowcol, counts, first_kind, second_kind, count):
    first = counts[first_kind]
    columns = []
    for e in range(count):
        slot_first = first_kind * CAP + min(e, CAP - 1)
        slot_second = second_kind * CAP + jnp.clip(e - first, 0, CAP - 1)
        columns.append(rowcol[1, jnp.where(e < first, slot_first, slot_second)])
    return columns


def kernel(
    layers,
    tile_devs,
    groups,
    rowcol_hbm,
    counts_hbm,
    src_hbm,
    green_hbm,
    out,
    state,
    recv,
    recv_whole,
    send,
    stage,
    weights,
    green,
    rowcol,
    counts,
    cols_next,
    counts_next,
    cols_prev,
    counts_prev,
    slot_of,
    entry_of,
    source_of,
    same,
    where_is,
    pack_of,
    local_sem,
    meta_send_sem,
    meta_recv_sem,
    send_sem,
    recv_sem,
):
    layer = lax.axis_index("layer")
    place = lax.axis_index("tile")
    up_ok, down_ok = layer > 0, layer < layers - 1
    low_ok, high_ok = place > 0, place < tile_devs - 1
    even = layer % 2 == 0

    lower, upper = layer + 1, layer - 1
    links = [
        (down_ok, (lower, place), up_ok),
        (down_ok & low_ok, (lower, place - 1), up_ok & high_ok),
        (down_ok & high_ok, (lower, place + 1), up_ok & low_ok),
        (up_ok, (upper, place), down_ok),
        (up_ok & low_ok, (upper, place - 1), down_ok & high_ok),
        (up_ok & high_ok, (upper, place + 1), down_ok & low_ok),
    ]

    barrier = pltpu.get_barrier_semaphore()
    for ok, device, _ in links:

        @pl.when(ok)
        def _(device=device):
            pl.semaphore_signal(barrier, inc=1, device_id=device, device_id_type=MESH)

    list_copies = [
        pltpu.make_async_copy(there, here, local_sem.at[2 * TILES_DEV + 1 + i])
        for i, (there, here) in enumerate(((rowcol_hbm, rowcol), (counts_hbm, counts)))
    ]
    for copy in list_copies:
        copy.start()
    src_copies = []
    for direction in range(2):
        for tile in range(TILES_DEV):
            copy = pltpu.make_async_copy(
                src_hbm.at[direction, :, :, pl.ds(tile * TILE, TILE)],
                state.at[SRC + direction * TILES_DEV + tile],
                local_sem.at[direction * TILES_DEV + tile],
            )
            copy.start()
            src_copies.append(copy)
    green_copy = pltpu.make_async_copy(green_hbm, green, local_sem.at[2 * TILES_DEV])
    green_copy.start()

    @pl.when(layer == 0)
    def _():
        recv_whole[0] = jnp.zeros((TILES_DEV, 2, GROUP, TILE), F32)

        @pl.loop(0, SWEEPS * groups)
        def _(i):
            recv[i // groups, i % groups, pl.ds(0, 16)] = jnp.zeros((16, 2, GROUP, TILE), F32)

    @pl.when(layer == layers - 1)
    def _():
        recv_whole[1] = jnp.zeros((TILES_DEV, 2, GROUP, TILE), F32)

        @pl.loop(0, SWEEPS * groups)
        def _(i):
            recv[i // groups, i % groups, pl.ds(16, 16)] = jnp.zeros((16, 2, GROUP, TILE), F32)

    sides = 1 + low_ok.astype(jnp.int32) + high_ok.astype(jnp.int32)
    ends = up_ok.astype(jnp.int32) + down_ok.astype(jnp.int32)
    for copy in list_copies:
        copy.wait()
    pl.semaphore_wait(barrier, sides * ends)

    def slot_lists(side, device):
        there = ((cols_next, counts_next), (cols_prev, counts_prev))[side]
        return [
            pltpu.make_async_remote_copy(
                here,
                there[i],
                meta_send_sem.at[side, i],
                meta_recv_sem.at[side, i],
                device_id=(device, place),
                device_id_type=MESH,
            )
            for i, here in enumerate((rowcol, counts))
        ]

    @pl.when(up_ok)
    def _():
        for copy in slot_lists(0, upper):
            copy.start()

    @pl.when(down_ok)
    def _():
        for copy in slot_lists(1, lower):
            copy.start()

    def message(k, g, q):
        direction, kind = q // 3, q % 3
        base = direction * 16
        count = OWN[direction] if kind == 0 else BAND
        if kind == 0:
            source = send.at[k, g, pl.ds(base, count)]
            target = base
        elif kind == 1:
            source = send.at[k, g, pl.ds(base + 8, count)]
            target = base + 12
        else:
            source = send.at[k, g, pl.ds(base + 12, count)]
            target = base + 8
        return pltpu.make_async_remote_copy(
            source,
            recv.at[k, g, pl.ds(target, count)],
            send_sem.at[k, g, q],
            recv_sem.at[k, g, q],
            device_id=links[q][1],
            device_id_type=MESH,
        )

    def first_halo(g, q):
        direction, kind = q // 3, q % 3
        base = direction * 16
        tile = SRC + base + (0 if kind == 1 else TILES_DEV - BAND)
        target = base + (12 if kind == 1 else 8)
        return pltpu.make_async_remote_copy(
            state.at[pl.ds(tile, BAND), :, pl.ds(pl.multiple_of(g * GROUP, GROUP), GROUP), :],
            recv.at[0, g, pl.ds(target, BAND)],
            send_sem.at[0, g, q],
            recv_sem.at[0, g, q],
            device_id=links[q][1],
            device_id_type=MESH,
        )

    for copy in src_copies:
        copy.wait()
    def first_own(direction):
        q = 3 * direction
        return pltpu.make_async_remote_copy(
            state.at[pl.ds(SRC + direction * TILES_DEV, TILES_DEV), :, pl.ds(0, GROUP), :],
            recv_whole.at[direction],
            send_sem.at[0, 0, q],
            recv_sem.at[0, 0, q],
            device_id=links[q][1],
            device_id_type=MESH,
        )

    for g in range(groups):
        for q in (1, 2, 4, 5):

            @pl.when(links[q][0])
            def _(g=g, q=q):
                first_halo(g, q).start()

        if g == 0:
            for direction in range(2):

                @pl.when(links[3 * direction][0])
                def _(direction=direction):
                    first_own(direction).start()

    c0, c1, c2, c3 = [counts[k] for k in range(4)]
    p1, p2, p3 = c0, c0 + c1, c0 + c1 + c2
    total = p3 + c3
    targets, lives = [], []
    for j in range(LIVE):
        in1, in2, in3 = j >= p1, j >= p2, j >= p3
        kind = in1.astype(jnp.int32) + in2.astype(jnp.int32) + in3.astype(jnp.int32)
        base = jnp.where(in3, p3, jnp.where(in2, p2, jnp.where(in1, p1, 0)))
        live = j < total
        slot = jnp.where(live, kind * CAP + j - base, 0)
        row = rowcol[0, slot] - place * TILES_DEV
        col = rowcol[1, slot] - place * TILES_DEV
        reads_up = in1 & jnp.logical_not(in3)
        own = j - base + jnp.where(in3, c0, jnp.where(in2, c1, 0))
        half = jnp.where(reads_up, 16, 0)
        halo = jnp.where(col < 0, 8 + BAND + col, 12 + col - TILES_DEV)
        inside = (col >= 0) & (col < TILES_DEV)
        target = row + jnp.where(in2, TILES_DEV, 0)
        slot_of[j] = slot
        entry_of[0, j] = jnp.where(live, half + jnp.where(inside, own, halo), 0)
        entry_of[1, j] = jnp.where(live, half + jnp.where(inside, 32 + col, halo), 32)
        source_of[j] = SRC + jnp.where(live, target, 0)
        targets.append(jnp.where(live, target, 64 + j))
        lives.append(live)
    for j in range(LIVE):
        same[j, j] = jnp.where(lives[j], 1.0, 0.0)
        for i in range(j):
            same[j, i] = jnp.where(targets[j] == targets[i], 1.0, 0.0)
    for r in range(2 * TILES_DEV):
        found = SRC + r
        for j in range(LIVE):
            found = jnp.where(targets[j] == r, j, found)
        where_is[r] = found

    @pl.when(up_ok)
    def _():
        for copy in slot_lists(0, upper):
            copy.wait_send()
        for copy in slot_lists(1, upper):
            copy.wait_recv()
        for e, column in enumerate(reader_columns(cols_prev, counts_prev, 1, 2, OWN[1])):
            pack_of[16 + e] = TILES_DEV + jnp.clip(column - place * TILES_DEV, 0, TILES_DEV - 1)

    @pl.when(down_ok)
    def _():
        for copy in slot_lists(1, lower):
            copy.wait_send()
        for copy in slot_lists(0, lower):
            copy.wait_recv()
        for e, column in enumerate(reader_columns(cols_next, counts_next, 0, 3, OWN[0])):
            pack_of[e] = jnp.clip(column - place * TILES_DEV, 0, TILES_DEV - 1)

    def shots_of(g):
        return pl.ds(pl.multiple_of(g * GROUP, GROUP), GROUP)

    def pack_own(k, g, index_of):
        for direction, ok in ((0, down_ok), (1, up_ok)):

            @pl.when(ok)
            def _(direction=direction):
                for e in range(OWN[direction]):
                    i = direction * 16 + e
                    send[k, g, i] = state[index_of(pack_of[i]), :, shots_of(g), :]
                message(k, g, direction * 3).start()

    @pl.loop(1, groups)
    def _(g):
        pack_own(0, g, lambda tile: SRC + tile)

    green_copy.wait()

    @pl.loop(0, LIVE)
    def _(j):
        blocks = green[slot_of[j]] * jnp.where(j < total, 1.0, 0.0)
        re, im = blocks[0], blocks[1]
        for column, part in enumerate((re.T, im.T)):
            high = part.astype(BF16)
            weights[j, :, pl.ds(column * TILE, TILE)] = high
            weights[j, :, pl.ds((2 + column) * TILE, TILE)] = (part - high.astype(F32)).astype(BF16)

    for direction in range(2):

        @pl.when(links[3 * direction][2])
        def _(direction=direction):
            first_own(direction).wait_recv()

        @pl.when(links[3 * direction][0])
        def _(direction=direction):
            first_own(direction).wait_send()

        stage[pl.ds(32 + direction * TILES_DEV, TILES_DEV)] = recv_whole[direction]

    def step(k, g):
        later = (k > 0) | (g > 0)
        whole = jnp.where(later, 0, 1)
        for q in range(6):

            @pl.when(links[q][0] & (later if q % 3 == 0 else True))
            def _(q=q):
                message(k, g, q).wait_send()

        for q in range(6):

            @pl.when(links[q][2] & (later if q % 3 == 0 else True))
            def _(q=q):
                message(k, g, q).wait_recv()

        stage[pl.ds(0, 32)] = recv[k, g]
        terms = []
        for j in range(LIVE):
            x = stage[entry_of[whole, j]]
            x = x.reshape(2 * GROUP, TILE)
            high = x.astype(BF16)
            both = jnp.concatenate([high, (x - high.astype(F32)).astype(BF16)], axis=0)
            p = lax.dot_general(both, weights[j], (((1,), (0,)), ((), ())), preferred_element_type=F32)
            p = p[:, : 2 * TILE] + p[:, 2 * TILE :]
            p = p[: 2 * GROUP] + p[2 * GROUP :]
            by_re, by_im = p[:, :TILE], p[:, TILE:]
            terms.append((by_re[:GROUP] - by_im[GROUP:], by_im[:GROUP] + by_re[GROUP:]))
        for j in range(LIVE):
            at = source_of[j]
            for part in range(2):
                acc = terms[j][part] + state[at, part, shots_of(g), :]
                for i in range(j):
                    acc = acc + same[j, i] * terms[i][part]
                state[j, part, shots_of(g), :] = acc

        @pl.when(k < SWEEPS - 1)
        def _():
            for direction, turn in ((1, even), (0, True), (1, jnp.logical_not(even))):
                for kind in (1, 2):
                    q = 3 * direction + kind

                    @pl.when(links[q][0] & turn)
                    def _(q=q, direction=direction, kind=kind):
                        first = 0 if kind == 1 else TILES_DEV - BAND
                        for e in range(BAND):
                            found = where_is[direction * TILES_DEV + first + e]
                            send[k + 1, g, direction * 16 + 4 + 4 * kind + e] = state[found, :, shots_of(g), :]
                        message(k + 1, g, q).start()

                @pl.when(links[3 * direction][0] & turn)
                def _(direction=direction):
                    for e in range(OWN[direction]):
                        i = direction * 16 + e
                        send[k + 1, g, i] = state[where_is[pack_of[i]], :, shots_of(g), :]
                    message(k + 1, g, direction * 3).start()

        @pl.when(k == SWEEPS - 1)
        def _():
            for r in range(2 * TILES_DEV):
                columns = pl.ds(r % TILES_DEV * TILE, TILE)
                out[r // TILES_DEV, :, shots_of(g), columns] = state[where_is[r], :, shots_of(g), :]

    @pl.loop(0, SWEEPS * groups)
    def _(i):
        step(i // groups, i % groups)


def body(layers, tile_devs, sources, green, rowcol, counts):
    shots, width = sources.shape[3], sources.shape[4]
    groups = shots // GROUP
    slots = green.shape[1]
    in_hbm = pl.BlockSpec(memory_space=pltpu.HBM)
    traces = pl.pallas_call(
        functools.partial(kernel, layers, tile_devs, groups),
        out_shape=jax.ShapeDtypeStruct((2, 2, shots, width), F32),
        in_specs=[in_hbm] * 4,
        out_specs=pl.BlockSpec(memory_space=pltpu.VMEM),
        scratch_shapes=[
            pltpu.VMEM((LIVE + 2 * TILES_DEV, 2, shots, TILE), F32),
            pltpu.VMEM((SWEEPS, groups, 32, 2, GROUP, TILE), F32),
            pltpu.VMEM((2, TILES_DEV, 2, GROUP, TILE), F32),
            pltpu.VMEM((SWEEPS, groups, 32, 2, GROUP, TILE), F32),
            pltpu.VMEM((64, 2, GROUP, TILE), F32),
            pltpu.VMEM((LIVE, TILE, 4 * TILE), BF16),
            pltpu.VMEM((slots, 2, TILE, TILE), F32),
            pltpu.SMEM((2, slots), jnp.int32),
            pltpu.SMEM((4,), jnp.int32),
            pltpu.SMEM((2, slots), jnp.int32),
            pltpu.SMEM((4,), jnp.int32),
            pltpu.SMEM((2, slots), jnp.int32),
            pltpu.SMEM((4,), jnp.int32),
            pltpu.SMEM((LIVE,), jnp.int32),
            pltpu.SMEM((2, LIVE), jnp.int32),
            pltpu.SMEM((LIVE,), jnp.int32),
            pltpu.SMEM((LIVE, LIVE), F32),
            pltpu.SMEM((2 * TILES_DEV,), jnp.int32),
            pltpu.SMEM((32,), jnp.int32),
            pltpu.SemaphoreType.DMA((2 * TILES_DEV + 3,)),
            pltpu.SemaphoreType.DMA((2, 2)),
            pltpu.SemaphoreType.DMA((2, 2)),
            pltpu.SemaphoreType.DMA((SWEEPS, groups, 6)),
            pltpu.SemaphoreType.DMA((SWEEPS, groups, 6)),
        ],
        compiler_params=pltpu.CompilerParams(collective_id=0, has_side_effects=True, vmem_limit_bytes=VMEM),
    )(*[pltpu.with_memory_space_constraint(x, pltpu.HBM) for x in (rowcol[0].T, counts[0], sources[0], green[0])])
    return traces[None]


def solution(mesh):
    return jax.shard_map(
        functools.partial(body, mesh.shape["layer"], mesh.shape["tile"]),
        mesh=mesh,
        in_specs=(
            P("layer", None, None, None, "tile"),
            P("layer", "tile", None, None, None),
            P("layer", "tile", None),
            P("layer", "tile"),
        ),
        out_specs=P("layer", None, None, None, "tile"),
        check_vma=False,
    )
```
